256 devices in a mesh: section: 8 (over x, y_hi), shard: 32 (over z, y_lo, core).
Axes of the slice: x: 4, y: 4 (y_hi: 2, y_lo: 2; y = y_hi * 2 + y_lo), z: 8, core: 2. Of those that a mesh axis runs over, the one named last changes fastest.
Arguments:
- rows: bfloat16 [8, 2048, 6144], P('section', 'shard'), may hold values from -6 to 6
- expert_ids: int32 [8, 2048, 2], P('section', 'shard'), may hold values from 0 to 7, all different within a row; in each aligned block of 64 rows (0 to 63, 64 to 127, ..., all dimensions but the last counted through in order) at most 18 rows name the same one
- gate_probs: float32 [8, 2048, 2], P('section', 'shard'), may hold values from 0.1 to 1
- w_gate: bfloat16 [8, 6144, 8192], P('section', None, 'shard'), may hold values from -0.078125 to 0.078125
- w_up: bfloat16 [8, 6144, 8192], P('section', None, 'shard'), may hold values from -0.078125 to 0.078125
- w_down: bfloat16 [8, 8192, 6144], P('section', 'shard'), may hold values from -0.0625 to 0.0625
Outputs:
- handed: bfloat16 [8, 2048, 6144], P('section', 'shard')
The draws below stay inside these ranges and needn't reach their ends.
Inputs may be any that keep to these rules, and one draw needn't show every extreme that they name: `expert_ids`: within each section's block of 64 tokens of one shard index, no expert is named by more than 18 tokens, and each token names 2 different experts.
All inputs are finite; a program needn't handle non-finite values.
Results may differ from the reference program's by a relative error of at most 0.011.
Values may be sent and summed in bfloat16 or wider, within the bound.
A program may use at most 128 MiB of HBM per device.

```python
import math
import jax
import jax.numpy as jnp
import numpy as np
from jax import lax

D = 6144
EXPERTS = 8
TOP = 2
FFW = 8192
TOK_DEV = 64
CAP = 18
TOK_SECTION = 2048
HID_DEV = 256
N_SECTION = 8
N_SHARD = 32


def level_of(stream_key, shape, split, least, high):
    def one(dim, parts):
        steps = jax.random.uniform(jax.random.fold_in(jax.random.fold_in(stream_key, 6), dim), (parts,), jnp.float32, least / len(split), high / len(split))
        return jnp.repeat(jnp.exp(steps), shape[dim] // parts).reshape((-1,) + (1,) * (len(shape) - dim - 1))

    level = one(*split[0])
    for cut in split[1:]:
        level = level * one(*cut)
    return level


def shared_out(key, own, number, rows, number_of, top, bound, slope):
    sequence = jax.random.permutation(key, number_of)
    crowded, usual = load_shares(number_of, rows * top, bound, slope, True), load_shares(number_of, rows * top, bound, slope, False)
    places = jnp.arange(number_of)

    def named(tallies, offset_by):
        used = int((tallies > 0).sum())
        fixed = max(1, used // 4)
        moved = fixed + (places - fixed + offset_by * (used - fixed)) % max(1, number_of - fixed)
        return jnp.zeros((number_of,), jnp.int32).at[sequence[jnp.where(places < fixed, places, moved)]].set(jnp.asarray(tallies, jnp.int32))

    tallies = jnp.where(number % 4 == 0, named(crowded, number // 4), named(usual, number - number // 4 - 1))
    mixed = jax.random.permutation(jax.random.fold_in(own, 3), number_of)
    donor, receiver = mixed[0:number_of // 2 * 2:2], mixed[1:number_of // 2 * 2:2]
    room = jnp.minimum(tallies[donor] - 1, bound - tallies[receiver]) // 2
    room = jnp.where((donor == sequence[0]) | (receiver == sequence[0]) | (tallies[receiver] == 0), 0, jnp.maximum(room, 0))
    moved = jax.random.randint(jax.random.fold_in(own, 4), (number_of // 2,), 0, 1 << 20) % (room + 1)
    tallies = tallies.at[donor].add(-moved).at[receiver].add(moved)
    members = jnp.searchsorted(jnp.cumsum(tallies), jnp.arange(rows * top), side="right").astype(jnp.int32)
    listing = members.reshape(top, rows).T
    listing = listing[jax.random.permutation(jax.random.fold_in(own, 1), rows)]
    offset_by = jax.random.randint(jax.random.fold_in(own, 2), (rows, 1), 0, top)
    return jnp.take_along_axis(listing, (jnp.arange(top)[None, :] + offset_by) % top, axis=1)


def load_shares(number_of, total, limit, skew, full):
    loads = [(1 << 20) // math.isqrt(standing ** skew) + 1 for standing in range(1, number_of + 1)]
    largest = limit if full else min(limit, max(-(-total // number_of), total * loads[0] // sum(loads)))
    least = 1 if total - largest >= number_of - 1 else 0
    counts, rest = [largest] + [least] * (number_of - 1), total - largest - least * (number_of - 1)
    while rest > 0:
        movable = [i for i in range(1, number_of) if counts[i] < largest] or [i for i in range(1, number_of) if counts[i] < limit]
        pool, left = sum([loads[i] for i in movable]), rest
        for i in movable:
            extra = min(limit - counts[i], max(1, left * loads[i] // pool), rest)
            counts[i] = counts[i] + extra
            rest = rest - extra
    return np.array(counts)


def noise(rng, extent, scale, limit, shards=(), held_as=jnp.bfloat16):
    loudness = level_of(rng, extent, shards, -0.22, 0.18) if shards else 1.0
    result = jax.random.normal(rng, extent, jnp.float32) * scale * loudness
    return jnp.minimum(jnp.maximum(result, -limit), limit).astype(held_as)


def setup_inputs(seed: int = 0) -> dict:
    key_of = jax.random.split(jax.random.key(seed), 7)
    rows = noise(key_of[0], (N_SECTION, TOK_SECTION, D), 1.0, 6.0, ((0, 8), (1, 32)))
    expert_ids_keys = jax.random.split(jax.random.fold_in(key_of[1], 1), N_SECTION * TOK_SECTION // TOK_DEV)
    expert_ids_turns = jax.random.permutation(jax.random.fold_in(key_of[1], 3), N_SECTION * TOK_SECTION // TOK_DEV)
    expert_ids = jax.vmap(lambda own, number: shared_out(jax.random.fold_in(key_of[1], 2), own, number, TOK_DEV, EXPERTS, TOP, CAP, 2))(expert_ids_keys, expert_ids_turns).reshape((N_SECTION, TOK_SECTION, TOP))
    gate_probs = jnp.clip(0.1 + 0.9 * jax.random.uniform(key_of[2], (N_SECTION, TOK_SECTION, TOP), jnp.float32) ** level_of(key_of[2], (N_SECTION, TOK_SECTION, TOP), ((0, 8), (1, 32)), -0.2, 0.2), 0.1, 1.0)
    w_gate = noise(key_of[3], (N_SECTION, D, FFW), D ** -0.5, 0.078125, ((0, 8), (2, 32)))
    w_up = noise(key_of[4], (N_SECTION, D, FFW), D ** -0.5, 0.078125, ((0, 8), (2, 32)))
    w_down = noise(key_of[5], (N_SECTION, FFW, D), FFW ** -0.5, 0.0625, ((0, 8), (1, 32)))
    return dict(rows=rows, expert_ids=expert_ids, gate_probs=gate_probs, w_gate=w_gate, w_up=w_up, w_down=w_down)


def section_layer(tokens, chosen_ids, probs, gate_w, up_w, down_w, section_num):
    hit = chosen_ids == section_num
    routed = jnp.any(hit, axis=-1)
    weight = jnp.sum(jnp.where(hit, probs, jnp.float32(0.0)), axis=-1).astype(jnp.float32)
    blocks = routed.reshape(N_SHARD, TOK_DEV).astype(jnp.int32)
    slot = jnp.cumsum(blocks, axis=1).astype(jnp.int32) - 1
    base = (jnp.arange(N_SHARD, dtype=jnp.int32) * CAP)[:, None]
    dest = jnp.where(blocks > 0, base + slot, N_SHARD * CAP).reshape(-1).astype(jnp.int32)
    packed = jnp.zeros((N_SHARD * CAP + 1, D), jnp.bfloat16).at[dest].set(tokens)[:-1]
    gate = jnp.dot(packed, gate_w, preferred_element_type=jnp.float32)
    upper = jnp.dot(packed, up_w, preferred_element_type=jnp.float32)
    hidden = (jax.nn.silu(gate) * upper).astype(jnp.bfloat16)
    hid_blocks = jnp.transpose(hidden.reshape(N_SHARD * CAP, N_SHARD, HID_DEV), (1, 0, 2))
    down_blocks = down_w.reshape(N_SHARD, HID_DEV, D)

    def add_block(total, pair):
        part = jnp.dot(pair[0], pair[1], preferred_element_type=jnp.float32).astype(jnp.bfloat16)
        part = lax.optimization_barrier(part)
        return total + part.astype(jnp.float32), None

    total, unused = lax.scan(add_block, jnp.zeros((N_SHARD * CAP, D), jnp.float32), (hid_blocks, down_blocks))
    expert_out = total.astype(jnp.bfloat16)
    extended = jnp.concatenate([expert_out, jnp.zeros((1, D), jnp.bfloat16)], axis=0)
    per_token = extended[dest]
    mixed = tokens.astype(jnp.float32) + weight[:, None] * per_token.astype(jnp.float32)
    return mixed.astype(jnp.bfloat16)


def reference(rows, expert_ids, gate_probs, w_gate, w_up, w_down):
    outputs = []
    for section_num in range(N_SECTION):
        outputs.append(section_layer(rows[section_num], expert_ids[section_num], gate_probs[section_num], w_gate[section_num], w_up[section_num], w_down[section_num], section_num))
    stacked = jnp.stack(outputs, axis=0)
    return jnp.roll(stacked, 1, axis=0)
```

```python
import functools

import jax
import jax.numpy as jnp
from jax import lax
from jax.experimental import pallas as pl
from jax.experimental.pallas import tpu as pltpu
from jax.sharding import PartitionSpec as P

F32 = jnp.float32
BF16 = jnp.bfloat16
MAIN = 16
EXTRA = 2
FOLD = MAIN // EXTRA
MESH = pl.DeviceIdType.MESH


class Chunk:
    def __init__(self, pair, folded, start, width, turn, offset):
        self.pair = pair
        self.folded = folded
        self.cols = pl.ds(start, width)
        self.start = start
        self.width = width
        self.turn = turn
        self.room = pl.ds(offset, width)


def plan(depth):
    unit = depth // 8
    singles = [Chunk(False, True, 0, unit, 1, 0), Chunk(False, False, 0, unit, -1, unit)]
    rest = (depth - unit) // 256
    count = 4 if rest >= 4 else 2
    pairs, at, offset = [], unit, 0
    for i in range(count):
        width = (rest // count + (1 if i < rest % count else 0)) * 256
        if i == count - 1:
            width = depth - at
        pairs.append(Chunk(True, False, at, width, 1 if i % 2 == 0 else -1, offset))
        at += width
        offset += width
    return singles, pairs


def iota(shape, dim):
    return lax.broadcasted_iota(jnp.int32, shape, dim)


def dot(a, b):
    return jnp.dot(a, b, preferred_element_type=F32)


def kernel(
    singles,
    pairs,
    rings,
    rows_hbm,
    ids_ref,
    probs_ref,
    wg_hbm,
    wu_hbm,
    wd_hbm,
    out_ref,
    rows_v,
    rows_p,
    wg,
    wu,
    wd,
    xg,
    xt,
    gacc,
    uacc,
    hid,
    part,
    pt,
    ring_pair,
    ring_one,
    cross_pair,
    cross_one,
    fin,
    eo_s,
    eot_s,
    eo_p,
    eot_p,
    meta_s,
    meta_p,
    send_sem,
    recv_sem,
    local_sem,
):
    tok, depth = rows_v.shape
    units = wg.shape[2]
    fold = depth // FOLD
    total = gacc.shape[0]
    section = lax.axis_index("section")
    sections = lax.axis_size("section")
    me = lax.axis_index("shard")
    core = lax.rem(me, 2)
    y = lax.rem(me // 2, 2)
    z = me // 4
    other = 1 - y

    def at_z(step):
        return lax.rem(z + step + rings, rings)

    def shard_of(zz, yy, cc):
        return {"shard": zz * 4 + yy * 2 + cc}

    following = {"section": lax.rem(section + 1, sections)}
    previous = {"section": lax.rem(section + sections - 1, sections)}
    across = shard_of(z, other, core)
    sibling = shard_of(z, y, 1 - core)
    up_z = shard_of(at_z(1), y, core)
    down_z = shard_of(at_z(-1), y, core)
    far = rings // 2
    hops = {1: far, -1: far - 1}

    used = []
    started = []

    def remote(src, dst, device):
        i = len(used)
        used.append(i)
        copy = pltpu.make_async_remote_copy(
            src_ref=src,
            dst_ref=dst,
            send_sem=send_sem.at[i],
            recv_sem=recv_sem.at[i],
            device_id=device,
            device_id_type=MESH,
        )
        copy.start()
        started.append(copy)
        return copy

    rows_in = pltpu.make_async_copy(rows_hbm.at[0], rows_v, local_sem.at[0])
    rows_in.start()
    own = [
        pltpu.make_async_copy(wg_hbm.at[0], wg.at[0], local_sem.at[1]),
        pltpu.make_async_copy(wu_hbm.at[0], wu.at[0], local_sem.at[2]),
        pltpu.make_async_copy(wd_hbm.at[0], wd.at[pl.ds(0, units)], local_sem.at[3]),
    ]
    for copy in own:
        copy.start()

    barrier = pltpu.get_barrier_semaphore()
    for device in (up_z, down_z, across, sibling, previous):
        pl.semaphore_signal(barrier, inc=1, device_id=device, device_id_type=MESH)

    hit = ids_ref[...] == section
    routed = jnp.max(jnp.where(hit, 1.0, 0.0).astype(F32), axis=0, keepdims=True)
    weight = jnp.sum(jnp.where(hit, probs_ref[...], 0.0), axis=0, keepdims=True)
    upper = (iota((tok, tok), 0) <= iota((tok, tok), 1)).astype(F32)
    count = dot(jnp.broadcast_to(routed, (8, tok)).astype(BF16), upper.astype(BF16))
    slot = jnp.where(routed > 0, count[0:1] - 1.0, -1.0)
    meta_s[...] = jnp.zeros_like(meta_s)
    meta_s[0:1, 0:tok] = slot
    meta_s[1:2, 0:tok] = weight
    place = iota((MAIN, tok), 0).astype(F32)
    placed = jnp.where(slot == place, 1.0, 0.0).astype(BF16)
    row16 = iota((MAIN, tok), 0)
    row_of = (MAIN + row16 // FOLD).astype(F32)

    rows_in.wait()
    pl.semaphore_wait(barrier, 5)

    weights = [
        remote(wg_hbm.at[0], wg.at[1], sibling),
        remote(wu_hbm.at[0], wu.at[1], sibling),
        remote(wd_hbm.at[0], wd.at[pl.ds(units, units)], sibling),
    ]

    def gathered(chunk):
        return xt if chunk.folded else xg

    ring = {}
    cross = {}

    def send_ring(chunk, hop):
        ref = gathered(chunk)
        for turn in (chunk.turn, -chunk.turn):
            if hop > hops[turn * chunk.turn]:
                continue
            held = at_z(-turn * (hop - 1))
            if chunk.pair:
                block = ref.at[:, held, :, chunk.cols]
            else:
                block = ref.at[y, held, :, chunk.cols]
            ring[chunk, turn, hop] = remote(block, block, up_z if turn == 1 else down_z)

    def send_across(chunk, held, key):
        block = gathered(chunk).at[y, held, :, chunk.cols]
        cross[chunk, key] = remote(block, block, across)

    for chunk in singles:
        if chunk.folded:
            folded = jnp.zeros((MAIN, fold), F32)
            for b in range(FOLD):
                pick = jnp.where((slot == row_of) & (row16 % FOLD == b), 1.0, 0.0)
                folded += dot(pick.astype(BF16), rows_v[:, b * fold : (b + 1) * fold])
            xt[y, z] = folded.astype(BF16)
        else:
            xg[y, z, :, chunk.cols] = dot(placed, rows_v[:, chunk.cols]).astype(BF16)
        send_ring(chunk, 1)
    for chunk in pairs:
        xg[y, z, :, chunk.cols] = dot(placed, rows_v[:, chunk.cols]).astype(BF16)
        send_across(chunk, z, 0)
    for chunk in singles:
        send_across(chunk, z, 0)
    for chunk in pairs:
        cross[chunk, 0].wait_recv()
        send_ring(chunk, 1)
    handed = [
        remote(rows_hbm.at[0], rows_p, following),
        remote(meta_s, meta_p, following),
    ]
    for hop in range(1, far + 1):
        for chunk in singles + pairs:
            for turn in (chunk.turn, -chunk.turn):
                if hop > hops[turn * chunk.turn]:
                    continue
                if hop == far and chunk.pair:
                    continue
                ring[chunk, turn, hop].wait_recv()
                if not chunk.pair:
                    send_across(chunk, at_z(-turn * hop), turn * hop)
            if hop < far:
                send_ring(chunk, hop + 1)

    for copy in own[:2]:
        copy.wait()
    for copy in weights[:2]:
        copy.wait_recv()

    def await_single(chunk):
        for key in list(cross):
            if key[0] is chunk:
                cross[key].wait_recv()

    def products(chunk, first):
        for i in range(2):
            to = pl.ds(i * units, units)
            for acc, w in ((gacc, wg), (uacc, wu)):
                x = xg[:, :, :, chunk.cols].reshape(total, chunk.width)
                made = dot(x, w[i, chunk.cols, :])
                if first:
                    acc[:, to] = made
                else:
                    acc[:, to] += made

    await_single(singles[0])
    lane = iota((MAIN, rings * MAIN), 1)
    line = iota((MAIN, rings * MAIN), 0)
    home = (line // EXTRA) * MAIN + (line % EXTRA) * FOLD
    for yy in range(2):
        block = xt[yy].reshape(rings * MAIN, fold)
        for b in range(FOLD):
            pick = jnp.where(lane == home + b, 1.0, 0.0).astype(BF16)
            xg[yy, rings, :, b * fold : (b + 1) * fold] = dot(pick, block).astype(BF16)
    await_single(singles[1])
    products(singles[1], True)
    for chunk in pairs:
        ring[chunk, chunk.turn, far].wait_recv()
        products(chunk, False)

    rows_at_once = 2 * MAIN
    for r in range(0, total, rows_at_once):
        g = gacc[r : r + rows_at_once, :]
        u = uacc[r : r + rows_at_once, :]
        hid[r : r + rows_at_once, :] = (g / (1.0 + jnp.exp(-g)) * u).astype(BF16)

    own[2].wait()
    weights[2].wait_recv()

    def down(chunk):
        step = 256
        for c in range(chunk.start, chunk.start + chunk.width, step):
            c1 = min(c + step, chunk.start + chunk.width)
            made = dot(hid[...], wd[:, c:c1]).astype(BF16)
            part[:, :, :, c:c1] = made.reshape(2, rings + 1, MAIN, c1 - c)

    def partial(chunk):
        return pt if chunk.folded else part

    sums = {}

    def slots(chunk):
        return ring_pair if chunk.pair else ring_one

    def index_of(chunk, turn, hop):
        return hop - 1 if turn == chunk.turn else far + hop - 1

    def send_sum(chunk, hop):
        ref = partial(chunk)
        for turn in (chunk.turn, -chunk.turn):
            last = hops[turn * chunk.turn]
            if hop > last:
                continue
            goal = at_z(turn * (last - hop + 1))
            i = index_of(chunk, turn, hop)
            if chunk.pair:
                src = ref.at[:, goal, :, chunk.cols]
                if hop > 1:
                    before = slots(chunk)[i - 1, :, :, chunk.room]
                    mine = ref[:, goal, :, chunk.cols]
                    ref[:, goal, :, chunk.cols] = (
                        mine.astype(F32) + before.astype(F32)
                    ).astype(BF16)
                dst = slots(chunk).at[i, :, :, chunk.room]
            else:
                src = ref.at[y, goal, :, chunk.cols]
                if hop > 1:
                    before = slots(chunk)[i - 1, :, chunk.room]
                    mine = ref[y, goal, :, chunk.cols]
                    ref[y, goal, :, chunk.cols] = (
                        mine.astype(F32) + before.astype(F32)
                    ).astype(BF16)
                dst = slots(chunk).at[i, :, chunk.room]
            sums[chunk, turn, hop] = remote(src, dst, up_z if turn == 1 else down_z)

    crossed = {}

    def cross_single(chunk):
        block = partial(chunk).at[other, pl.ds(0, rings), :, chunk.cols]
        crossed[chunk] = remote(block, cross_one.at[:, :, chunk.room], across)

    down(singles[1])
    cross_single(singles[1])
    for chunk in pairs:
        down(chunk)
        send_sum(chunk, 1)
    spot = iota((rings * MAIN, MAIN), 0)
    line = iota((rings * MAIN, MAIN), 1)
    home = (line // EXTRA) * MAIN + (line % EXTRA) * FOLD
    for yy in range(2):
        block = jnp.zeros((rings * MAIN, fold), F32)
        for b in range(FOLD):
            pick = jnp.where(spot == home + b, 1.0, 0.0).astype(BF16)
            block += dot(pick, part[yy, rings, :, b * fold : (b + 1) * fold])
        pt[yy] = block.astype(BF16).reshape(rings, MAIN, fold)
    cross_single(singles[0])
    for chunk in (singles[1], singles[0]):
        crossed[chunk].wait_recv()
        ref = partial(chunk)
        for zz in range(rings):
            ref[y, zz, :, chunk.cols] = (
                ref[y, zz, :, chunk.cols].astype(F32)
                + cross_one[zz, :, chunk.room].astype(F32)
            ).astype(BF16)
        send_sum(chunk, 1)
    for hop in range(2, far + 1):
        for chunk in pairs + [singles[1], singles[0]]:
            for turn in (chunk.turn, -chunk.turn):
                if (chunk, turn, hop - 1) in sums:
                    if hop - 1 < hops[turn * chunk.turn]:
                        sums[chunk, turn, hop - 1].wait_recv()
            send_sum(chunk, hop)

    arrive = []

    def finish(chunk):
        for turn in (chunk.turn, -chunk.turn):
            sums[chunk, turn, hops[turn * chunk.turn]].wait_recv()
        ends = [
            index_of(chunk, chunk.turn, hops[1]),
            index_of(chunk, -chunk.turn, hops[-1]),
        ]
        return ends

    def pass_on(chunk):
        if chunk.folded:
            arrive.append(remote(eot_s, eot_p, following))
        else:
            block = eo_s.at[:, chunk.cols]
            arrive.append(remote(block, eo_p.at[:, chunk.cols], following))

    for chunk in pairs:
        ends = finish(chunk)
        for yy, keep in ((other, False), (y, True)):
            made = part[yy, z, :, chunk.cols].astype(F32)
            for i in ends:
                made += ring_pair[i, yy, :, chunk.room].astype(F32)
            if keep:
                fin[:, chunk.room] = made
            else:
                part[yy, z, :, chunk.cols] = made.astype(BF16)
                block = part.at[yy, z, :, chunk.cols]
                crossed[chunk] = remote(block, cross_pair.at[:, chunk.room], across)
    for chunk in (singles[1], singles[0]):
        ends = finish(chunk)
        made = partial(chunk)[y, z, :, chunk.cols].astype(F32)
        for i in ends:
            made += ring_one[i, :, chunk.room].astype(F32)
        if chunk.folded:
            eot_s[...] = made.astype(BF16)
        else:
            eo_s[:, chunk.cols] = made.astype(BF16)
        pass_on(chunk)
    for chunk in pairs:
        crossed[chunk].wait_recv()
        made = fin[:, chunk.room] + cross_pair[:, chunk.room].astype(F32)
        eo_s[:, chunk.cols] = made.astype(BF16)
        pass_on(chunk)

    for copy in handed:
        copy.wait_recv()
    diagonal = iota((tok, tok), 0) == iota((tok, tok), 1)

    def upright(i):
        line = jnp.broadcast_to(meta_p[i : i + 1, 0:tok], (tok, tok))
        return jnp.sum(jnp.where(diagonal, line, 0.0), axis=1, keepdims=True)

    slot_p = upright(0)
    weight_p = upright(1)
    spot = iota((tok, MAIN), 1)
    taken = jnp.where(slot_p == spot.astype(F32), 1.0, 0.0).astype(BF16)
    extra_of = (MAIN + spot // FOLD).astype(F32)
    for copy in arrive[:2]:
        copy.wait_recv()
    for b in range(FOLD):
        at = pl.ds(b * fold, fold)
        for copy, chunk in zip(arrive[2:], pairs):
            begins = chunk.start
            if b * fold <= begins < (b + 1) * fold:
                copy.wait_recv()
        pick = jnp.where((slot_p == extra_of) & (spot % FOLD == b), 1.0, 0.0)
        added = dot(taken, eo_p[:, at]) + dot(pick.astype(BF16), eot_p[...])
        out_ref[0, :, at] = (rows_p[:, at].astype(F32) + weight_p * added).astype(BF16)

    for copy in started:
        copy.wait_send()


def on_device(rows, expert_ids, gate_probs, w_gate, w_up, w_down):
    _, tok, depth = rows.shape
    units = w_gate.shape[2]
    rings = lax.axis_size("shard") // 4
    singles, pairs = plan(depth)
    fold = depth // FOLD
    total = 2 * (rings + 1) * MAIN
    wide = sum(c.width for c in pairs)
    thin = sum(c.width for c in singles)
    steps = rings - 1
    copies = 5
    copies += len(singles) * (steps + rings) + len(pairs) * (steps + 1)
    copies += len(singles) * (steps + 1) + len(pairs) * (steps + 1)
    copies += len(singles) + len(pairs)
    ids = jnp.transpose(expert_ids[0])
    probs = jnp.transpose(gate_probs[0])
    hbm = pl.BlockSpec(memory_space=pltpu.MemorySpace.HBM)
    vmem = pl.BlockSpec(memory_space=pltpu.MemorySpace.VMEM)
    return pl.pallas_call(
        functools.partial(kernel, singles, pairs, rings),
        out_shape=jax.ShapeDtypeStruct(rows.shape, BF16),
        in_specs=[hbm, vmem, vmem, hbm, hbm, hbm],
        out_specs=vmem,
        scratch_shapes=[
            pltpu.VMEM((tok, depth), BF16),
            pltpu.VMEM((tok, depth), BF16),
            pltpu.VMEM((2, depth, units), BF16),
            pltpu.VMEM((2, depth, units), BF16),
            pltpu.VMEM((2 * units, depth), BF16),
            pltpu.VMEM((2, rings + 1, MAIN, depth), BF16),
            pltpu.VMEM((2, rings, MAIN, fold), BF16),
            pltpu.VMEM((total, 2 * units), F32),
            pltpu.VMEM((total, 2 * units), F32),
            pltpu.VMEM((total, 2 * units), BF16),
            pltpu.VMEM((2, rings + 1, MAIN, depth), BF16),
            pltpu.VMEM((2, rings, MAIN, fold), BF16),
            pltpu.VMEM((steps, 2, MAIN, wide), BF16),
            pltpu.VMEM((steps, MAIN, thin), BF16),
            pltpu.VMEM((MAIN, wide), BF16),
            pltpu.VMEM((rings, MAIN, thin), BF16),
            pltpu.VMEM((MAIN, wide), F32),
            pltpu.VMEM((MAIN, depth), BF16),
            pltpu.VMEM((MAIN, fold), BF16),
            pltpu.VMEM((MAIN, depth), BF16),
            pltpu.VMEM((MAIN, fold), BF16),
            pltpu.VMEM((8, 128), F32),
            pltpu.VMEM((8, 128), F32),
            pltpu.SemaphoreType.DMA((copies,)),
            pltpu.SemaphoreType.DMA((copies,)),
            pltpu.SemaphoreType.DMA((4,)),
        ],
        compiler_params=pltpu.CompilerParams(
            collective_id=0, has_side_effects=True, vmem_limit_bytes=56 << 20
        ),
    )(rows, ids, probs, w_gate, w_up, w_down)


def solution(mesh):
    in_specs = (
        P("section", "shard", None),
        P("section", "shard", None),
        P("section", "shard", None),
        P("section", None, "shard"),
        P("section", None, "shard"),
        P("section", "shard", None),
    )
    out_specs = P("section", "shard", None)
    return jax.shard_map(
        on_device, mesh=mesh, in_specs=in_specs, out_specs=out_specs, check_vma=False
    )
```

```python
import functools

import jax
import jax.numpy as jnp
from jax import lax
from jax.experimental import pallas as pl
from jax.experimental.pallas import tpu as pltpu
from jax.sharding import PartitionSpec as P

F32 = jnp.float32
BF16 = jnp.bfloat16
MAIN = 16
EXTRA = 2
FOLD = MAIN // EXTRA
LANES = 256
MESH = pl.DeviceIdType.MESH


class Chunk:
    def __init__(self, pair, folded, start, width, turn, offset):
        self.pair = pair
        self.folded = folded
        self.cols = pl.ds(start, width)
        self.start = start
        self.width = width
        self.turn = turn
        self.room = pl.ds(offset, width)


GATHER = (2, 4, True)
REDUCE = (3, 4, False)
LAG = 1


def plan(depth, mains, shared, paired):
    unit = depth // FOLD
    singles, pairs = [], []
    thin = wide = at = 0
    if paired:
        pairs.append(Chunk(True, True, 0, unit, 1, 0))
        wide += unit
    else:
        singles.append(Chunk(False, True, 0, unit, 1, 0))
        thin += unit
    for i in range(mains):
        singles.append(Chunk(False, False, at, unit, -1 if i % 2 == 0 else 1, thin))
        at += unit
        thin += unit
    lines = (depth - at) // LANES
    for i in range(shared):
        width = (lines // shared + (1 if i < lines % shared else 0)) * LANES
        turn = 1 if (i + paired) % 2 == 0 else -1
        pairs.append(Chunk(True, False, at, width, turn, wide))
        at += width
        wide += width
    return singles, pairs


def iota(shape, dim):
    return lax.broadcasted_iota(jnp.int32, shape, dim)


def dot(a, b):
    return jnp.dot(a, b, preferred_element_type=F32)


def kernel(
    gather_plan,
    reduce_plan,
    rings,
    rows_hbm,
    ids_ref,
    probs_ref,
    wg_hbm,
    wu_hbm,
    wd_hbm,
    rows_p,
    eo_p,
    eot_p,
    meta_p,
    rows_v,
    wg,
    wu,
    wd,
    xg,
    xt,
    gacc,
    uacc,
    hid,
    part,
    pt,
    ring_pair,
    ring_one,
    cross_one,
    ends_s,
    eot_s,
    meta_s,
    send_sem,
    recv_sem,
    local_sem,
):
    singles, pairs = gather_plan
    tok, depth = rows_v.shape
    units = wg.shape[2]
    fold = depth // FOLD
    total = gacc.shape[0]
    section = lax.axis_index("section")
    sections = lax.axis_size("section")
    me = lax.axis_index("shard")
    core = lax.rem(me, 2)
    y = lax.rem(me // 2, 2)
    z = me // 4
    other = 1 - y

    def at_z(step):
        return lax.rem(z + step + rings, rings)

    def shard_of(zz, yy, cc):
        return {"shard": zz * 4 + yy * 2 + cc}

    following = {"section": lax.rem(section + 1, sections)}
    previous = {"section": lax.rem(section + sections - 1, sections)}
    across = shard_of(z, other, core)
    beside = {**following, **across}
    behind = {**previous, **across}
    sibling = shard_of(z, y, 1 - core)
    up_z = shard_of(at_z(1), y, core)
    down_z = shard_of(at_z(-1), y, core)
    far = rings // 2
    hops = {1: far, -1: far - 1}

    used = []
    started = []

    def remote(src, dst, device):
        i = len(used)
        used.append(i)
        copy = pltpu.make_async_remote_copy(
            src_ref=src,
            dst_ref=dst,
            send_sem=send_sem.at[i],
            recv_sem=recv_sem.at[i],
            device_id=device,
            device_id_type=MESH,
        )
        copy.start()
        started.append(copy)
        return copy

    rows_in = pltpu.make_async_copy(rows_hbm.at[0], rows_v, local_sem.at[0])
    rows_in.start()
    own = [
        pltpu.make_async_copy(wg_hbm.at[0], wg.at[0], local_sem.at[1]),
        pltpu.make_async_copy(wu_hbm.at[0], wu.at[0], local_sem.at[2]),
        pltpu.make_async_copy(wd_hbm.at[0], wd.at[pl.ds(0, units)], local_sem.at[3]),
    ]
    for copy in own:
        copy.start()

    barrier = pltpu.get_barrier_semaphore()
    for device in (up_z, down_z, across, sibling, previous, behind):
        pl.semaphore_signal(barrier, inc=1, device_id=device, device_id_type=MESH)

    hit = ids_ref[...] == section
    routed = jnp.max(jnp.where(hit, 1.0, 0.0).astype(F32), axis=0, keepdims=True)
    weight = jnp.sum(jnp.where(hit, probs_ref[...], 0.0), axis=0, keepdims=True)
    upper = (iota((tok, tok), 0) <= iota((tok, tok), 1)).astype(F32)
    count = dot(jnp.broadcast_to(routed, (8, tok)).astype(BF16), upper.astype(BF16))
    slot = jnp.where(routed > 0, count[0:1] - 1.0, -1.0)
    meta_s[...] = jnp.zeros_like(meta_s)
    meta_s[0:1, 0:tok] = slot
    meta_s[1:2, 0:tok] = weight
    place = iota((MAIN, tok), 0).astype(F32)
    placed = jnp.where(slot == place, 1.0, 0.0).astype(BF16)
    row16 = iota((MAIN, tok), 0)
    row_of = (MAIN + row16 // FOLD).astype(F32)

    def gathered(chunk):
        return xt if chunk.folded else xg

    rows_in.wait()
    for chunk in singles + pairs:
        if chunk.folded:
            folded = jnp.zeros((MAIN, fold), F32)
            for b in range(FOLD):
                pick = jnp.where((slot == row_of) & (row16 % FOLD == b), 1.0, 0.0)
                folded += dot(pick.astype(BF16), rows_v[:, b * fold : (b + 1) * fold])
            xt[y, z] = folded.astype(BF16)
        else:
            xg[y, z, :, chunk.cols] = dot(placed, rows_v[:, chunk.cols]).astype(BF16)

    pl.semaphore_wait(barrier, 6)
    weights = [
        remote(wg_hbm.at[0], wg.at[1], sibling),
        remote(wu_hbm.at[0], wu.at[1], sibling),
        remote(wd_hbm.at[0], wd.at[pl.ds(units, units)], sibling),
    ]

    ring = {}
    cross = {}

    def send_ring(chunk, hop, planes=None):
        ref = gathered(chunk)
        for turn in (chunk.turn, -chunk.turn):
            if hop > hops[turn * chunk.turn]:
                continue
            held = at_z(-turn * (hop - 1))
            if planes is None:
                block = ref.at[:, held, :, chunk.cols]
            else:
                block = ref.at[planes, held, :, chunk.cols]
            copy = remote(block, block, up_z if turn == 1 else down_z)
            ring.setdefault((chunk, turn, hop), []).append(copy)

    def await_ring(chunk, turn, hop):
        for copy in ring[chunk, turn, hop]:
            copy.wait_recv()

    def send_across(chunk, held, key):
        block = gathered(chunk).at[y, held, :, chunk.cols]
        cross[chunk, key] = remote(block, block, across)

    def advance(chunk, hop):
        for turn in (chunk.turn, -chunk.turn):
            if hop > hops[turn * chunk.turn]:
                continue
            await_ring(chunk, turn, hop)
            if not chunk.pair:
                send_across(chunk, at_z(-turn * hop), turn * hop)
        if hop < far:
            send_ring(chunk, hop + 1, None if chunk.pair else y)

    for chunk in singles:
        send_ring(chunk, 1, y)
    for chunk in pairs:
        send_across(chunk, z, 0)
        send_ring(chunk, 1, y)
    for chunk in singles:
        send_across(chunk, z, 0)
    for chunk in pairs:
        cross[chunk, 0].wait_recv()
        send_ring(chunk, 1, other)
    handed = [
        remote(rows_v, rows_p, following),
        remote(meta_s, meta_p, following),
    ]
    for hop in range(1, far):
        for chunk in singles:
            advance(chunk, hop)
        for chunk in pairs:
            advance(chunk, hop)

    for chunk in singles:
        advance(chunk, far)
    for copy in own[:2]:
        copy.wait()
    for copy in weights[:2]:
        copy.wait_recv()

    def await_single(chunk):
        for key in list(cross):
            if key[0] is chunk:
                cross[key].wait_recv()

    written = []

    def products(chunk):
        if chunk.pair:
            await_ring(chunk, chunk.turn, far)
        else:
            await_single(chunk)
        if chunk.folded:
            tail_rows()
            return
        for i in range(2):
            to = pl.ds(i * units, units)
            for acc, w in ((gacc, wg), (uacc, wu)):
                x = xg[:, :, :, chunk.cols].reshape(total, chunk.width)
                made = dot(x, w[i, chunk.cols, :])
                if written:
                    acc[:, to] += made
                else:
                    acc[:, to] = made
        written.append(chunk)

    def tail_rows():
        lane = iota((MAIN, rings * MAIN), 1)
        line = iota((MAIN, rings * MAIN), 0)
        home = (line // EXTRA) * MAIN + (line % EXTRA) * FOLD
        for yy in range(2):
            block = xt[yy].reshape(rings * MAIN, fold)
            for b in range(FOLD):
                pick = jnp.where(lane == home + b, 1.0, 0.0).astype(BF16)
                to = pl.ds(b * fold, fold)
                xg[yy, rings, :, to] = dot(pick, block).astype(BF16)

    folded_first = [c for c in singles + pairs if c.folded]
    mains_of = [c for c in singles if not c.folded]
    for chunk in folded_first + [c for c in pairs if not c.folded] + mains_of:
        products(chunk)

    rows_at_once = 2 * MAIN
    for r in range(0, total, rows_at_once):
        g = gacc[r : r + rows_at_once, :]
        u = uacc[r : r + rows_at_once, :]
        hid[r : r + rows_at_once, :] = (g / (1.0 + jnp.exp(-g)) * u).astype(BF16)

    singles, pairs = reduce_plan
    own[2].wait()
    weights[2].wait_recv()

    def down(chunk):
        step = 256
        for c in range(chunk.start, chunk.start + chunk.width, step):
            c1 = min(c + step, chunk.start + chunk.width)
            made = dot(hid[...], wd[:, c:c1]).astype(BF16)
            part[:, :, :, c:c1] = made.reshape(2, rings + 1, MAIN, c1 - c)

    def partial(chunk):
        return pt if chunk.folded else part

    sums = {}

    def slots(chunk):
        return ring_pair if chunk.pair else ring_one

    def index_of(chunk, turn, hop):
        return hop - 1 if turn == chunk.turn else far + hop - 1

    def send_sum(chunk, hop):
        ref = partial(chunk)
        for turn in (chunk.turn, -chunk.turn):
            last = hops[turn * chunk.turn]
            if hop > last:
                continue
            goal = at_z(turn * (last - hop + 1))
            i = index_of(chunk, turn, hop)
            if chunk.pair:
                src = ref.at[:, goal, :, chunk.cols]
                if hop > 1:
                    before = slots(chunk)[i - 1, :, :, chunk.room]
                    mine = ref[:, goal, :, chunk.cols]
                    ref[:, goal, :, chunk.cols] = (
                        mine.astype(F32) + before.astype(F32)
                    ).astype(BF16)
                dst = slots(chunk).at[i, :, :, chunk.room]
            else:
                src = ref.at[y, goal, :, chunk.cols]
                take_cross(chunk, turn * (last - hop + 1))
                if hop > 1:
                    before = slots(chunk)[i - 1, :, chunk.room]
                    mine = ref[y, goal, :, chunk.cols]
                    ref[y, goal, :, chunk.cols] = (
                        mine.astype(F32) + before.astype(F32)
                    ).astype(BF16)
                dst = slots(chunk).at[i, :, chunk.room]
            sums[chunk, turn, hop] = remote(src, dst, up_z if turn == 1 else down_z)

    crossed = {}

    def cross_single(chunk):
        for hop in range(1, far + 1):
            for turn in (chunk.turn, -chunk.turn):
                last = hops[turn * chunk.turn]
                if hop > last:
                    continue
                goal = at_z(turn * (last - hop + 1))
                block = partial(chunk).at[other, goal, :, chunk.cols]
                to = cross_one.at[goal, :, chunk.room]
                crossed[chunk, turn * (last - hop + 1)] = remote(block, to, across)
        block = partial(chunk).at[other, z, :, chunk.cols]
        crossed[chunk, 0] = remote(block, cross_one.at[z, :, chunk.room], across)

    def take_cross(chunk, step):
        crossed[chunk, step].wait_recv()
        ref, goal = partial(chunk), at_z(step)
        ref[y, goal, :, chunk.cols] = (
            ref[y, goal, :, chunk.cols].astype(F32)
            + cross_one[goal, :, chunk.room].astype(F32)
        ).astype(BF16)

    ones = singles[1:] + singles[:1]
    down(pairs[0])
    send_sum(pairs[0], 1)
    for chunk in singles[1:]:
        down(chunk)
        cross_single(chunk)
    for chunk in pairs[1:]:
        down(chunk)
        send_sum(chunk, 1)
    spot = iota((rings * MAIN, MAIN), 0)
    line = iota((rings * MAIN, MAIN), 1)
    home = (line // EXTRA) * MAIN + (line % EXTRA) * FOLD
    for yy in range(2):
        block = jnp.zeros((rings * MAIN, fold), F32)
        for b in range(FOLD):
            pick = jnp.where(spot == home + b, 1.0, 0.0).astype(BF16)
            block += dot(pick, part[yy, rings, :, b * fold : (b + 1) * fold])
        pt[yy] = block.astype(BF16).reshape(rings, MAIN, fold)
    cross_single(singles[0])

    def add(chunk, hop):
        for turn in (chunk.turn, -chunk.turn):
            if 1 < hop <= hops[turn * chunk.turn]:
                sums[chunk, turn, hop - 1].wait_recv()
        send_sum(chunk, hop)

    arrive = []

    def finish(chunk):
        for turn in (chunk.turn, -chunk.turn):
            sums[chunk, turn, hops[turn * chunk.turn]].wait_recv()
        ends = [
            index_of(chunk, chunk.turn, hops[1]),
            index_of(chunk, -chunk.turn, hops[-1]),
        ]
        return ends

    def finish_pair(chunk):
        ends = finish(chunk)
        for i, plane, device in ((1, other, beside), (0, y, following)):
            made = part[plane, z, :, chunk.cols].astype(F32)
            for end in ends:
                made += ring_pair[end, plane, :, chunk.room].astype(F32)
            ends_s[i, :, chunk.cols] = made.astype(BF16)
            block = ends_s.at[i, :, chunk.cols]
            arrive.append(remote(block, eo_p.at[i, :, chunk.cols], device))

    def finish_one(chunk):
        take_cross(chunk, 0)
        ends = finish(chunk)
        made = partial(chunk)[y, z, :, chunk.cols].astype(F32)
        for end in ends:
            made += ring_one[end, :, chunk.room].astype(F32)
        if chunk.folded:
            eot_s[...] = made.astype(BF16)
            arrive.append(remote(eot_s, eot_p, following))
        else:
            ends_s[0, :, chunk.cols] = made.astype(BF16)
            block = ends_s.at[0, :, chunk.cols]
            arrive.append(remote(block, eo_p.at[0, :, chunk.cols], following))

    for step in range(2, far + LAG + 2):
        behind_by = step - LAG
        for chunk in pairs:
            if step <= far:
                add(chunk, step)
            elif step == far + 1:
                finish_pair(chunk)
        for chunk in ones:
            if 1 <= behind_by <= far:
                add(chunk, behind_by)
            elif behind_by == far + 1:
                finish_one(chunk)

    for copy in handed + arrive:
        copy.wait_recv()
    for copy in started:
        copy.wait_send()
    assert len(used) == send_sem.shape[0]


def combine(singles, pairs, rows_p, eo_p, eot_p, meta_p, out_ref, made, done):
    tok, depth = rows_p.shape
    fold = depth // FOLD
    diagonal = iota((tok, tok), 0) == iota((tok, tok), 1)

    def upright(i):
        line = jnp.broadcast_to(meta_p[i : i + 1, 0:tok], (tok, tok))
        return jnp.sum(jnp.where(diagonal, line, 0.0), axis=1, keepdims=True)

    slot_p = upright(0)
    weight_p = upright(1)
    spot = iota((tok, MAIN), 1)
    taken = jnp.where(slot_p == spot.astype(F32), 1.0, 0.0).astype(BF16)
    extra_of = (MAIN + spot // FOLD).astype(F32)
    copies = []
    for b in range(FOLD):
        at = pl.ds(b * fold, fold)
        pick = jnp.where((slot_p == extra_of) & (spot % FOLD == b), 1.0, 0.0)
        added = dot(taken, eo_p[0, :, at]) + dot(pick.astype(BF16), eot_p[...])
        if b * fold >= pairs[0].start:
            added += dot(taken, eo_p[1, :, at])
        made[:, at] = (rows_p[:, at].astype(F32) + weight_p * added).astype(BF16)
        copies.append(pltpu.make_async_copy(made.at[:, at], out_ref.at[0, :, at], done.at[b]))
        copies[-1].start()
    for copy in copies:
        copy.wait()


def on_device(rows, expert_ids, gate_probs, w_gate, w_up, w_down):
    _, tok, depth = rows.shape
    units = w_gate.shape[2]
    rings = lax.axis_size("shard") // 4
    gather_plan, reduce_plan = plan(depth, *GATHER), plan(depth, *REDUCE)
    singles, pairs = gather_plan
    fold = depth // FOLD
    total = 2 * (rings + 1) * MAIN
    steps = rings - 1
    copies = 5
    copies += len(singles) * (steps + rings) + len(pairs) * (steps + 3)
    singles, pairs = reduce_plan
    copies += len(singles) * (steps + rings) + len(pairs) * steps
    copies += len(singles) + 2 * len(pairs)
    wide = sum(c.width for c in pairs)
    thin = sum(c.width for c in singles)
    ids = jnp.transpose(expert_ids[0])
    probs = jnp.transpose(gate_probs[0])
    hbm = pl.BlockSpec(memory_space=pltpu.MemorySpace.HBM)
    vmem = pl.BlockSpec(memory_space=pltpu.MemorySpace.VMEM)
    handed = pl.pallas_call(
        functools.partial(kernel, gather_plan, reduce_plan, rings),
        out_shape=[
            pltpu.VMEM((tok, depth), BF16),
            pltpu.VMEM((2, MAIN, depth), BF16),
            pltpu.VMEM((MAIN, fold), BF16),
            pltpu.VMEM((8, 128), F32),
        ],
        in_specs=[hbm, vmem, vmem, hbm, hbm, hbm],
        out_specs=[vmem] * 4,
        scratch_shapes=[
            pltpu.VMEM((tok, depth), BF16),
            pltpu.VMEM((2, depth, units), BF16),
            pltpu.VMEM((2, depth, units), BF16),
            pltpu.VMEM((2 * units, depth), BF16),
            pltpu.VMEM((2, rings + 1, MAIN, depth), BF16),
            pltpu.VMEM((2, rings, MAIN, fold), BF16),
            pltpu.VMEM((total, 2 * units), F32),
            pltpu.VMEM((total, 2 * units), F32),
            pltpu.VMEM((total, 2 * units), BF16),
            pltpu.VMEM((2, rings + 1, MAIN, depth), BF16),
            pltpu.VMEM((2, rings, MAIN, fold), BF16),
            pltpu.VMEM((steps, 2, MAIN, wide), BF16),
            pltpu.VMEM((steps, MAIN, thin), BF16),
            pltpu.VMEM((rings, MAIN, thin), BF16),
            pltpu.VMEM((2, MAIN, depth), BF16),
            pltpu.VMEM((MAIN, fold), BF16),
            pltpu.VMEM((8, 128), F32),
            pltpu.SemaphoreType.DMA((copies,)),
            pltpu.SemaphoreType.DMA((copies,)),
            pltpu.SemaphoreType.DMA((4,)),
        ],
        compiler_params=pltpu.CompilerParams(
            collective_id=0, has_side_effects=True, vmem_limit_bytes=58 << 20
        ),
    )(rows, ids, probs, w_gate, w_up, w_down)
    return pl.pallas_call(
        functools.partial(combine, singles, pairs),
        out_shape=jax.ShapeDtypeStruct(rows.shape, BF16),
        in_specs=[vmem] * 4,
        out_specs=hbm,
        scratch_shapes=[
            pltpu.VMEM((tok, depth), BF16),
            pltpu.SemaphoreType.DMA((FOLD,)),
        ],
        compiler_params=pltpu.CompilerParams(vmem_limit_bytes=8 << 20),
    )(*handed)


def solution(mesh):
    in_specs = (
        P("section", "shard", None),
        P("section", "shard", None),
        P("section", "shard", None),
        P("section", None, "shard"),
        P("section", None, "shard"),
        P("section", "shard", None),
    )
    out_specs = P("section", "shard", None)
    return jax.shard_map(
        on_device, mesh=mesh, in_specs=in_specs, out_specs=out_specs, check_vma=False
    )
```

```python
import functools

import jax
import jax.numpy as jnp
from jax import lax
from jax.experimental import pallas as pl
from jax.experimental.pallas import tpu as pltpu
from jax.sharding import PartitionSpec as P

F32 = jnp.float32
BF16 = jnp.bfloat16
MAIN = 16
EXTRA = 2
FOLD = MAIN // EXTRA
LANES = 256
MESH = pl.DeviceIdType.MESH


class Chunk:
    def __init__(self, pair, folded, start, width, turn, offset):
        self.pair = pair
        self.folded = folded
        self.cols = pl.ds(start, width)
        self.start = start
        self.width = width
        self.turn = turn
        self.room = pl.ds(offset, width)


GATHER = (2, 4, True)
REDUCE = (4, 4, False)
LAG = 1


def plan(depth, mains, shared, paired):
    unit = depth // FOLD
    singles, pairs = [], []
    lines = (depth - mains * unit) // LANES
    load = {1: 0, -1: 0}
    held = {True: 0, False: 0}

    def make(pair, folded, start, width):
        turn = 1 if load[1] <= load[-1] else -1
        load[turn] += width * (2 if pair else 1)
        (pairs if pair else singles).append(Chunk(pair, folded, start, width, turn, held[pair]))
        held[pair] += width

    if paired:
        make(True, True, 0, unit)
    at = mains * unit
    for i in range(shared):
        width = (lines // shared + (1 if i < lines % shared else 0)) * LANES
        make(True, False, at, width)
        at += width
    if not paired:
        make(False, True, 0, unit)
    for i in range(mains):
        make(False, False, i * unit, unit)
    return singles, pairs


def iota(shape, dim):
    return lax.broadcasted_iota(jnp.int32, shape, dim)


def dot(a, b):
    return jnp.dot(a, b, preferred_element_type=F32)


def kernel(
    gather_plan,
    reduce_plan,
    rings,
    rows_hbm,
    ids_ref,
    probs_ref,
    wg_hbm,
    wu_hbm,
    wd_hbm,
    rows_p,
    eo_p,
    eot_p,
    meta_p,
    rows_v,
    wg,
    wu,
    wd,
    xg,
    xt,
    gacc,
    uacc,
    hid,
    part,
    pt,
    ring_pair,
    ring_one,
    cross_one,
    ends_s,
    eot_s,
    meta_s,
    send_sem,
    recv_sem,
    local_sem,
):
    singles, pairs = gather_plan
    tok, depth = rows_v.shape
    units = wg.shape[2]
    fold = depth // FOLD
    total = gacc.shape[0]
    section = lax.axis_index("section")
    sections = lax.axis_size("section")
    me = lax.axis_index("shard")
    core = lax.rem(me, 2)
    y = lax.rem(me // 2, 2)
    z = me // 4
    other = 1 - y

    def at_z(step):
        return lax.rem(z + step + rings, rings)

    def shard_of(zz, yy, cc):
        return {"shard": zz * 4 + yy * 2 + cc}

    following = {"section": lax.rem(section + 1, sections)}
    previous = {"section": lax.rem(section + sections - 1, sections)}
    across = shard_of(z, other, core)
    beside = {**following, **across}
    behind = {**previous, **across}
    sibling = shard_of(z, y, 1 - core)
    up_z = shard_of(at_z(1), y, core)
    down_z = shard_of(at_z(-1), y, core)
    far = rings // 2
    hops = {1: far, -1: far - 1}

    used = []
    started = []

    def remote(src, dst, device):
        i = len(used)
        used.append(i)
        copy = pltpu.make_async_remote_copy(
            src_ref=src,
            dst_ref=dst,
            send_sem=send_sem.at[i],
            recv_sem=recv_sem.at[i],
            device_id=device,
            device_id_type=MESH,
        )
        copy.start()
        started.append(copy)
        return copy

    rows_in = pltpu.make_async_copy(rows_hbm.at[0], rows_v, local_sem.at[0])
    rows_in.start()
    own = [
        pltpu.make_async_copy(wg_hbm.at[0], wg.at[0], local_sem.at[1]),
        pltpu.make_async_copy(wu_hbm.at[0], wu.at[0], local_sem.at[2]),
        pltpu.make_async_copy(wd_hbm.at[0], wd.at[pl.ds(0, units)], local_sem.at[3]),
    ]
    for copy in own:
        copy.start()

    barrier = pltpu.get_barrier_semaphore()
    for device in (up_z, down_z, across, sibling, previous, behind):
        pl.semaphore_signal(barrier, inc=1, device_id=device, device_id_type=MESH)

    hit = ids_ref[...] == section
    routed = jnp.max(jnp.where(hit, 1.0, 0.0).astype(F32), axis=0, keepdims=True)
    weight = jnp.sum(jnp.where(hit, probs_ref[...], 0.0), axis=0, keepdims=True)
    upper = (iota((tok, tok), 0) <= iota((tok, tok), 1)).astype(F32)
    count = dot(jnp.broadcast_to(routed, (8, tok)).astype(BF16), upper.astype(BF16))
    slot = jnp.where(routed > 0, count[0:1] - 1.0, -1.0)
    meta_s[...] = jnp.zeros_like(meta_s)
    meta_s[0:1, 0:tok] = slot
    meta_s[1:2, 0:tok] = weight
    place = iota((MAIN, tok), 0).astype(F32)
    placed = jnp.where(slot == place, 1.0, 0.0).astype(BF16)
    row16 = iota((MAIN, tok), 0)
    row_of = (MAIN + row16 // FOLD).astype(F32)

    def gathered(chunk):
        return xt if chunk.folded else xg

    rows_in.wait()
    for chunk in singles + pairs:
        if chunk.folded:
            folded = jnp.zeros((MAIN, fold), F32)
            for b in range(FOLD):
                pick = jnp.where((slot == row_of) & (row16 % FOLD == b), 1.0, 0.0)
                folded += dot(pick.astype(BF16), rows_v[:, b * fold : (b + 1) * fold])
            xt[y, z] = folded.astype(BF16)
        else:
            xg[y, z, :, chunk.cols] = dot(placed, rows_v[:, chunk.cols]).astype(BF16)

    pl.semaphore_wait(barrier, 6)
    weights = [
        remote(wg_hbm.at[0], wg.at[1], sibling),
        remote(wu_hbm.at[0], wu.at[1], sibling),
        remote(wd_hbm.at[0], wd.at[pl.ds(units, units)], sibling),
    ]

    ring = {}
    cross = {}

    def send_ring(chunk, hop, planes=None):
        ref = gathered(chunk)
        for turn in (chunk.turn, -chunk.turn):
            if hop > hops[turn * chunk.turn]:
                continue
            held = at_z(-turn * (hop - 1))
            if planes is None:
                block = ref.at[:, held, :, chunk.cols]
            else:
                block = ref.at[planes, held, :, chunk.cols]
            copy = remote(block, block, up_z if turn == 1 else down_z)
            ring.setdefault((chunk, turn, hop), []).append(copy)

    def await_ring(chunk, turn, hop):
        for copy in ring[chunk, turn, hop]:
            copy.wait_recv()

    def send_across(chunk, held, key):
        block = gathered(chunk).at[y, held, :, chunk.cols]
        cross[chunk, key] = remote(block, block, across)

    def advance(chunk, hop):
        for turn in (chunk.turn, -chunk.turn):
            if hop > hops[turn * chunk.turn]:
                continue
            await_ring(chunk, turn, hop)
            if not chunk.pair:
                send_across(chunk, at_z(-turn * hop), turn * hop)
        if hop < far:
            send_ring(chunk, hop + 1, None if chunk.pair else y)

    for chunk in singles:
        send_ring(chunk, 1, y)
    for chunk in pairs:
        send_across(chunk, z, 0)
        send_ring(chunk, 1, y)
    for chunk in singles:
        send_across(chunk, z, 0)
    for chunk in pairs:
        cross[chunk, 0].wait_recv()
        send_ring(chunk, 1, other)
    handed = [
        remote(rows_v, rows_p, following),
        remote(meta_s, meta_p, following),
    ]
    for hop in range(1, far):
        for chunk in singles:
            advance(chunk, hop)
        for chunk in pairs:
            advance(chunk, hop)

    for chunk in singles:
        advance(chunk, far)
    for copy in own[:2]:
        copy.wait()
    for copy in weights[:2]:
        copy.wait_recv()

    def await_single(chunk):
        for key in list(cross):
            if key[0] is chunk:
                cross[key].wait_recv()

    written = []

    def products(chunk):
        if chunk.pair:
            await_ring(chunk, chunk.turn, far)
        else:
            await_single(chunk)
        if chunk.folded:
            tail_rows()
            return
        for i in range(2):
            to = pl.ds(i * units, units)
            for acc, w in ((gacc, wg), (uacc, wu)):
                x = xg[:, :, :, chunk.cols].reshape(total, chunk.width)
                made = dot(x, w[i, chunk.cols, :])
                if written:
                    acc[:, to] += made
                else:
                    acc[:, to] = made
        written.append(chunk)

    def tail_rows():
        lane = iota((MAIN, rings * MAIN), 1)
        line = iota((MAIN, rings * MAIN), 0)
        home = (line // EXTRA) * MAIN + (line % EXTRA) * FOLD
        for yy in range(2):
            block = xt[yy].reshape(rings * MAIN, fold)
            for b in range(FOLD):
                pick = jnp.where(lane == home + b, 1.0, 0.0).astype(BF16)
                to = pl.ds(b * fold, fold)
                xg[yy, rings, :, to] = dot(pick, block).astype(BF16)

    folded_first = [c for c in singles + pairs if c.folded]
    mains_of = [c for c in singles if not c.folded]
    for chunk in folded_first + [c for c in pairs if not c.folded] + mains_of:
        products(chunk)

    rows_at_once = 2 * MAIN
    for r in range(0, total, rows_at_once):
        g = gacc[r : r + rows_at_once, :]
        u = uacc[r : r + rows_at_once, :]
        hid[r : r + rows_at_once, :] = (g / (1.0 + jnp.exp(-g)) * u).astype(BF16)

    singles, pairs = reduce_plan
    own[2].wait()
    weights[2].wait_recv()

    def down(chunk):
        step = 256
        for c in range(chunk.start, chunk.start + chunk.width, step):
            c1 = min(c + step, chunk.start + chunk.width)
            made = dot(hid[...], wd[:, c:c1]).astype(BF16)
            part[:, :, :, c:c1] = made.reshape(2, rings + 1, MAIN, c1 - c)

    def partial(chunk):
        return pt if chunk.folded else part

    sums = {}

    def slots(chunk):
        return ring_pair if chunk.pair else ring_one

    def index_of(chunk, turn, hop):
        return hop - 1 if turn == chunk.turn else far + hop - 1

    def send_sum(chunk, hop):
        ref = partial(chunk)
        for turn in (chunk.turn, -chunk.turn):
            last = hops[turn * chunk.turn]
            if hop > last:
                continue
            goal = at_z(turn * (last - hop + 1))
            i = index_of(chunk, turn, hop)
            if chunk.pair:
                src = ref.at[:, goal, :, chunk.cols]
                if hop > 1:
                    before = slots(chunk)[i - 1, :, :, chunk.room]
                    mine = ref[:, goal, :, chunk.cols]
                    ref[:, goal, :, chunk.cols] = (
                        mine.astype(F32) + before.astype(F32)
                    ).astype(BF16)
                dst = slots(chunk).at[i, :, :, chunk.room]
            else:
                src = ref.at[y, goal, :, chunk.cols]
                take_cross(chunk, turn * (last - hop + 1))
                if hop > 1:
                    before = slots(chunk)[i - 1, :, chunk.room]
                    mine = ref[y, goal, :, chunk.cols]
                    ref[y, goal, :, chunk.cols] = (
                        mine.astype(F32) + before.astype(F32)
                    ).astype(BF16)
                dst = slots(chunk).at[i, :, chunk.room]
            sums[chunk, turn, hop] = remote(src, dst, up_z if turn == 1 else down_z)

    crossed = {}

    def cross_single(chunk, hop):
        steps = []
        for turn in (chunk.turn, -chunk.turn):
            last = hops[turn * chunk.turn]
            if hop <= last:
                steps.append(turn * (last - hop + 1))
        for step in steps or [0]:
            goal = at_z(step)
            block = partial(chunk).at[other, goal, :, chunk.cols]
            to = cross_one.at[goal, :, chunk.room]
            crossed[chunk, step] = remote(block, to, across)

    def take_cross(chunk, step):
        crossed[chunk, step].wait_recv()
        ref, goal = partial(chunk), at_z(step)
        ref[y, goal, :, chunk.cols] = (
            ref[y, goal, :, chunk.cols].astype(F32)
            + cross_one[goal, :, chunk.room].astype(F32)
        ).astype(BF16)

    ones = singles[1:] + singles[:1]
    down(pairs[0])
    send_sum(pairs[0], 1)
    for chunk in singles[1:]:
        down(chunk)
        cross_single(chunk, 1)
    for chunk in pairs[1:]:
        down(chunk)
        send_sum(chunk, 1)
    spot = iota((rings * MAIN, MAIN), 0)
    line = iota((rings * MAIN, MAIN), 1)
    home = (line // EXTRA) * MAIN + (line % EXTRA) * FOLD
    for yy in range(2):
        block = jnp.zeros((rings * MAIN, fold), F32)
        for b in range(FOLD):
            pick = jnp.where(spot == home + b, 1.0, 0.0).astype(BF16)
            block += dot(pick, part[yy, rings, :, b * fold : (b + 1) * fold])
        pt[yy] = block.astype(BF16).reshape(rings, MAIN, fold)
    cross_single(singles[0], 1)
    for hop in range(2, far + 2):
        for chunk in ones:
            cross_single(chunk, hop)

    def add(chunk, hop):
        for turn in (chunk.turn, -chunk.turn):
            if 1 < hop <= hops[turn * chunk.turn]:
                sums[chunk, turn, hop - 1].wait_recv()
        send_sum(chunk, hop)

    arrive = []

    def finish(chunk):
        for turn in (chunk.turn, -chunk.turn):
            sums[chunk, turn, hops[turn * chunk.turn]].wait_recv()
        ends = [
            index_of(chunk, chunk.turn, hops[1]),
            index_of(chunk, -chunk.turn, hops[-1]),
        ]
        return ends

    def finish_pair(chunk):
        ends = finish(chunk)
        for i, plane, device in ((1, other, beside), (0, y, following)):
            made = part[plane, z, :, chunk.cols].astype(F32)
            for end in ends:
                made += ring_pair[end, plane, :, chunk.room].astype(F32)
            ends_s[i, :, chunk.cols] = made.astype(BF16)
            block = ends_s.at[i, :, chunk.cols]
            arrive.append(remote(block, eo_p.at[i, :, chunk.cols], device))

    def finish_one(chunk):
        take_cross(chunk, 0)
        ends = finish(chunk)
        made = partial(chunk)[y, z, :, chunk.cols].astype(F32)
        for end in ends:
            made += ring_one[end, :, chunk.room].astype(F32)
        if chunk.folded:
            eot_s[...] = made.astype(BF16)
            arrive.append(remote(eot_s, eot_p, following))
        else:
            ends_s[0, :, chunk.cols] = made.astype(BF16)
            block = ends_s.at[0, :, chunk.cols]
            arrive.append(remote(block, eo_p.at[0, :, chunk.cols], following))

    for step in range(2, far + LAG + 2):
        behind_by = step - LAG
        for chunk in pairs:
            if step <= far:
                add(chunk, step)
            elif step == far + 1:
                finish_pair(chunk)
        for chunk in ones:
            if 1 <= behind_by <= far:
                add(chunk, behind_by)
            elif behind_by == far + 1:
                finish_one(chunk)

    for copy in handed + arrive:
        copy.wait_recv()
    for copy in started:
        copy.wait_send()
    assert len(used) == send_sem.shape[0]


def combine(singles, pairs, rows_p, eo_p, eot_p, meta_p, out_ref, made, done):
    tok, depth = rows_p.shape
    fold = depth // FOLD
    diagonal = iota((tok, tok), 0) == iota((tok, tok), 1)

    def upright(i):
        line = jnp.broadcast_to(meta_p[i : i + 1, 0:tok], (tok, tok))
        return jnp.sum(jnp.where(diagonal, line, 0.0), axis=1, keepdims=True)

    slot_p = upright(0)
    weight_p = upright(1)
    spot = iota((tok, MAIN), 1)
    taken = jnp.where(slot_p == spot.astype(F32), 1.0, 0.0).astype(BF16)
    extra_of = (MAIN + spot // FOLD).astype(F32)
    copies = []
    for b in range(FOLD):
        at = pl.ds(b * fold, fold)
        pick = jnp.where((slot_p == extra_of) & (spot % FOLD == b), 1.0, 0.0)
        added = dot(taken, eo_p[0, :, at]) + dot(pick.astype(BF16), eot_p[...])
        if b * fold >= pairs[0].start:
            added += dot(taken, eo_p[1, :, at])
        made[:, at] = (rows_p[:, at].astype(F32) + weight_p * added).astype(BF16)
        copies.append(pltpu.make_async_copy(made.at[:, at], out_ref.at[0, :, at], done.at[b]))
        copies[-1].start()
    for copy in copies:
        copy.wait()


def on_device(rows, expert_ids, gate_probs, w_gate, w_up, w_down):
    _, tok, depth = rows.shape
    units = w_gate.shape[2]
    rings = lax.axis_size("shard") // 4
    gather_plan, reduce_plan = plan(depth, *GATHER), plan(depth, *REDUCE)
    singles, pairs = gather_plan
    fold = depth // FOLD
    total = 2 * (rings + 1) * MAIN
    steps = rings - 1
    copies = 5
    copies += len(singles) * (steps + rings) + len(pairs) * (steps + 3)
    singles, pairs = reduce_plan
    copies += len(singles) * (steps + rings) + len(pairs) * steps
    copies += len(singles) + 2 * len(pairs)
    wide = sum(c.width for c in pairs)
    thin = sum(c.width for c in singles)
    ids = jnp.transpose(expert_ids[0])
    probs = jnp.transpose(gate_probs[0])
    hbm = pl.BlockSpec(memory_space=pltpu.MemorySpace.HBM)
    vmem = pl.BlockSpec(memory_space=pltpu.MemorySpace.VMEM)
    handed = pl.pallas_call(
        functools.partial(kernel, gather_plan, reduce_plan, rings),
        out_shape=[
            pltpu.VMEM((tok, depth), BF16),
            pltpu.VMEM((2, MAIN, depth), BF16),
            pltpu.VMEM((MAIN, fold), BF16),
            pltpu.VMEM((8, 128), F32),
        ],
        in_specs=[hbm, vmem, vmem, hbm, hbm, hbm],
        out_specs=[vmem] * 4,
        scratch_shapes=[
            pltpu.VMEM((tok, depth), BF16),
            pltpu.VMEM((2, depth, units), BF16),
            pltpu.VMEM((2, depth, units), BF16),
            pltpu.VMEM((2 * units, depth), BF16),
            pltpu.VMEM((2, rings + 1, MAIN, depth), BF16),
            pltpu.VMEM((2, rings, MAIN, fold), BF16),
            pltpu.VMEM((total, 2 * units), F32),
            pltpu.VMEM((total, 2 * units), F32),
            pltpu.VMEM((total, 2 * units), BF16),
            pltpu.VMEM((2, rings + 1, MAIN, depth), BF16),
            pltpu.VMEM((2, rings, MAIN, fold), BF16),
            pltpu.VMEM((steps, 2, MAIN, wide), BF16),
            pltpu.VMEM((steps, MAIN, thin), BF16),
            pltpu.VMEM((rings, MAIN, thin), BF16),
            pltpu.VMEM((2, MAIN, depth), BF16),
            pltpu.VMEM((MAIN, fold), BF16),
            pltpu.VMEM((8, 128), F32),
            pltpu.SemaphoreType.DMA((copies,)),
            pltpu.SemaphoreType.DMA((copies,)),
            pltpu.SemaphoreType.DMA((4,)),
        ],
        compiler_params=pltpu.CompilerParams(
            collective_id=0, has_side_effects=True, vmem_limit_bytes=58 << 20
        ),
    )(rows, ids, probs, w_gate, w_up, w_down)
    return pl.pallas_call(
        functools.partial(combine, singles, pairs),
        out_shape=jax.ShapeDtypeStruct(rows.shape, BF16),
        in_specs=[vmem] * 4,
        out_specs=hbm,
        scratch_shapes=[
            pltpu.VMEM((tok, depth), BF16),
            pltpu.SemaphoreType.DMA((FOLD,)),
        ],
        compiler_params=pltpu.CompilerParams(vmem_limit_bytes=8 << 20),
    )(*handed)


def solution(mesh):
    in_specs = (
        P("section", "shard", None),
        P("section", "shard", None),
        P("section", "shard", None),
        P("section", None, "shard"),
        P("section", None, "shard"),
        P("section", "shard", None),
    )
    out_specs = P("section", "shard", None)
    return jax.shard_map(
        on_device, mesh=mesh, in_specs=in_specs, out_specs=out_specs, check_vma=False
    )
```
